32 devices in a mesh: dp: 4 (over z), mx: 2 (over y), my: 4 (over x, core).
Axes of the slice: x: 2, y: 2, z: 4, core: 2. Of those that a mesh axis runs over, the one named last changes fastest.
Arguments:
- stream_in: bfloat16 [4096, 1600], P(('dp', 'mx'), 'my'), may hold values from -60 to 60, as said below
- seg_ids: int32 [16, 256], P(('dp', 'my')), may hold values from 0 to 15, never falling along the last dimension, each value on 1 to 128 neighbouring positions
- gain_first: float32 [1600], P('my'), may hold values from 0.5 to 1.5
- shift_first: float32 [1600], P('my'), may hold values from -1.5 to 1.5
- w_qkv: bfloat16 [1600, 3, 2048], P('my', None, 'mx'), may hold values from -1 to 1
- qkv_bias: float32 [2, 2048], P(None, 'mx'), may hold values from -2.5 to 2.5
- w_proj: bfloat16 [2048, 1600], P('mx', 'my'), may hold values from -1 to 1
- proj_bias: float32 [1600], P('my'), may hold values from -1.5 to 1.5
- gain_second: float32 [1600], P('my'), may hold values from 0.5 to 1.5
- shift_second: float32 [1600], P('my'), may hold values from -1.5 to 1.5
- w_up: bfloat16 [1600, 6400], P('my', 'mx'), may hold values from -0.15625 to 0.15625
- up_bias: float32 [6400], P('mx'), may hold values from -1.5 to 1.5
- w_down: bfloat16 [6400, 1600], P('mx', 'my'), may hold values from -0.078125 to 0.078125
- down_bias: float32 [1600], P('my'), may hold values from -1.5 to 1.5
- cotangent: bfloat16 [4096, 1600], P(('dp', 'mx'), 'my'), may hold values from -6 to 6
Outputs:
- block_out: bfloat16 [4096, 1600], P(('dp', 'mx'), 'my')
- grad_stream: float32 [4096, 1600], P(('dp', 'mx'), 'my')
- grad_gain_first: float32 [1600], P('my')
- grad_shift_first: float32 [1600], P('my')
- grad_w_qkv: float32 [1600, 3, 2048], P('my', None, 'mx')
- grad_qkv_bias: float32 [2, 2048], P(None, 'mx')
- grad_w_proj: float32 [2048, 1600], P('mx', 'my')
- grad_proj_bias: float32 [1600], P('my')
- grad_gain_second: float32 [1600], P('my')
- grad_shift_second: float32 [1600], P('my')
- grad_w_up: float32 [1600, 6400], P('my', 'mx')
- grad_up_bias: float32 [6400], P('mx')
- grad_w_down: float32 [6400, 1600], P('mx', 'my')
- grad_down_bias: float32 [1600], P('my')
The draws below stay inside these ranges and needn't reach their ends.
Inputs may be any that keep to these rules, and one draw needn't show every extreme that they name: `seg_ids`: segment numbers never fall along a sequence; a segment spans 1 to 128 positions. `stream_in`: entries of the block's input.
All inputs are finite; a program needn't handle non-finite values.
Results may differ from the reference program's by a relative error of at most 0.011.
Values may be sent and summed in bfloat16 or wider, within the bound.
No kernel may reach another device: no remote copies, remote signals or barrier semaphores. Data moves between devices by JAX's collectives and lax.ppermute only.
A program may use at most 192 MiB of HBM per device.

```python
import math
import jax
import jax.numpy as jnp
import numpy as np
from jax import lax

D = 1600
FF = 6400
NH = 25
HD = 64
HP = 32
LEN = 256
SEGS = 16
MOST = 128
SEQS = 16
TOKENS = 4096


def draw_stream_in(key, part):
    keys_all = jax.random.split(jax.random.fold_in(key, 11), 2)
    column = jnp.arange(D, dtype=jnp.float32)
    rising = 0.5 + 1.5 * column / D
    roughness = jnp.exp(jax.random.uniform(keys_all[1], (D,), minval=-0.4, maxval=0.4))
    values = jax.random.truncated_normal(keys_all[0], -6.0, 6.0, (TOKENS, D)) * rising * roughness
    return jnp.clip(values, -60.0, 60.0).astype(jnp.bfloat16)


def draw_w_qkv(key, part):
    base_key = jax.random.fold_in(key, 23)
    fan_scale = D ** (-0.5)
    values = jax.random.truncated_normal(base_key, -4.0, 4.0, (D, 3, HP * HD)) * fan_scale
    return jnp.clip(values, -1.0, 1.0).astype(jnp.bfloat16)


def level_of(key, shape, pieces, low, largest):
    gain, own = 1.0, jax.random.fold_in(key, 6)
    for axis_at, parts in pieces:
        draws = jnp.exp(jax.random.uniform(jax.random.fold_in(own, axis_at), (parts,), jnp.float32, low / len(pieces), largest / len(pieces)))
        gain = gain * jnp.repeat(draws, shape[axis_at] // parts).reshape([-1 if axis == axis_at else 1 for axis in range(len(shape))])
    return gain


def length_profile(amount, total, most, skew):
    weights = [(1 << 20) // math.isqrt(standing ** skew) + 1 for standing in range(2, amount + 1)]
    rest, counts = total - most - (amount - 1), [1] * (amount - 1)
    while rest > 0:
        candidates = [i for i in range(amount - 1) if counts[i] < most]
        whole, remaining = sum([weights[i] for i in candidates]), rest
        for i in candidates:
            addition = min(most - counts[i], max(1, remaining * weights[i] // whole), rest)
            counts[i] = counts[i] + addition
            rest = rest - addition
    return np.array([most] + counts)


def ragged(key, amount, total, bound, skew):
    if amount == 2:
        one = jax.random.randint(key, (), max(1, total - bound), min(bound, total - 1) + 1)
        return jnp.stack([one, total - one])
    lengths = jnp.asarray(length_profile(amount, total, bound, skew), jnp.int32)
    couples = (amount - 1) // 2
    source_of, taker = lengths[1:1 + 2 * couples:2], lengths[2:2 + 2 * couples:2]
    room = jnp.minimum(source_of - 1, bound - taker)
    shifted = jax.random.randint(jax.random.fold_in(key, 1), (couples,), 0, 1 << 20) % (room + 1)
    lengths = lengths.at[1:1 + 2 * couples:2].set(source_of - shifted).at[2:2 + 2 * couples:2].set(taker + shifted)
    return lengths[jax.random.permutation(jax.random.fold_in(key, 2), amount)]


def scatter_about(stream_key, extent, width, reach, cuts=(), kind=jnp.bfloat16):
    values = width * jax.random.normal(stream_key, extent, jnp.float32)
    if cuts:
        values = values * level_of(stream_key, extent, cuts, -0.22, 0.18)
    return jnp.clip(values, -reach, reach).astype(kind)


def setup_inputs(seed: int = 0) -> dict:
    seeds = jax.random.split(jax.random.key(seed), 16)
    return {
        "stream_in": draw_stream_in(jax.random.fold_in(seeds[15], 71), 0),
        "seg_ids": jax.vmap(lambda own: jnp.searchsorted(jnp.cumsum(ragged(own, SEGS, LEN, MOST, 2)), jnp.arange(LEN), side="right"))(jax.random.split(seeds[1], SEQS)).reshape((SEQS, LEN)).astype(jnp.int32),
        "gain_first": jnp.clip(1.0 + 0.1 * jax.random.normal(seeds[2], (D,), jnp.float32), 0.5, 1.5),
        "shift_first": scatter_about(seeds[3], (D,), 0.3, 1.5, ((0, 4),), jnp.float32),
        "w_qkv": draw_w_qkv(jax.random.fold_in(seeds[15], 71), 0),
        "qkv_bias": scatter_about(seeds[5], (2, HP * HD), 0.5, 2.5, ((1, 2),), jnp.float32),
        "w_proj": scatter_about(seeds[6], (HP * HD, D), (HP * HD // 64) ** -0.5, 1.0, ((0, 2), (1, 4))),
        "proj_bias": scatter_about(seeds[7], (D,), 0.3, 1.5, ((0, 4),), jnp.float32),
        "gain_second": jnp.clip(1.0 + 0.1 * jax.random.normal(seeds[8], (D,), jnp.float32), 0.5, 1.5),
        "shift_second": scatter_about(seeds[9], (D,), 0.3, 1.5, ((0, 4),), jnp.float32),
        "w_up": scatter_about(seeds[10], (D, FF), D ** -0.5, 0.15625, ((0, 4), (1, 2))),
        "up_bias": scatter_about(seeds[11], (FF,), 0.3, 1.5, ((0, 2),), jnp.float32),
        "w_down": scatter_about(seeds[12], (FF, D), FF ** -0.5, 0.078125, ((0, 2), (1, 4))),
        "down_bias": scatter_about(seeds[13], (D,), 0.3, 1.5, ((0, 4),), jnp.float32),
        "cotangent": scatter_about(seeds[14], (TOKENS, D), 1.0, 6.0, ((0, 8), (1, 4))),
    }


@jax.custom_vjp
def low(v):
    return lax.optimization_barrier(v.astype(jnp.bfloat16)).astype(jnp.float32)

@jax.custom_vjp
def low_back(v):
    return v

def low_keep(v):
    return (low(v), None)

def low_pass(kept, grad):
    return (grad,)

def back_keep(v):
    return (v, None)

def back_low(kept, grad):
    return (low(grad),)
low.defvjp(low_keep, low_pass)
low_back.defvjp(back_keep, back_low)

def both_ways(values):
    return low(low_back(values))

def layer_norm(stream, gain_vec, shift_vec):
    row_mean = lax.optimization_barrier(jnp.mean(stream, axis=-1, keepdims=True))
    centred = stream - row_mean
    variance = lax.optimization_barrier(jnp.mean(centred * centred, axis=-1, keepdims=True))
    return centred * lax.rsqrt(variance + 1e-05) * gain_vec + shift_vec

def attend_one(seq_block):
    queries, key_in, values, segment = seq_block
    highest = lax.Precision.HIGHEST
    q_heads = queries.reshape(LEN, HP, HD)
    k_heads = key_in.reshape(LEN, HP, HD)
    v_heads = values.reshape(LEN, HP, HD)
    scores = low_back(jnp.einsum('qhd,khd->hqk', q_heads, k_heads, precision=highest) * HD ** (-0.5))
    position = jnp.arange(LEN)
    allowed = (position[:, None] >= position[None, :]) & (segment[:, None] == segment[None, :])
    scores = jnp.where(allowed[None], scores, -jnp.inf)
    attn_weights = low(jax.nn.softmax(scores, axis=-1))
    attended = jnp.einsum('hqk,khd->qhd', attn_weights, v_heads, precision=highest)
    return attended.reshape(LEN, HP * HD)

def forward(stream, gain_first, shift_first, w_qkv, qkv_bias, w_proj, proj_bias, gain_second, shift_second, w_up, up_bias, w_down, down_bias, seg_ids):
    highest = lax.Precision.HIGHEST
    live_cols = (jnp.arange(HP * HD) // HD < NH).astype(jnp.float32)
    entry_one = low(layer_norm(stream, gain_first, shift_first))
    mixed_qkv = jnp.einsum('td,dkc->tkc', entry_one, w_qkv * live_cols, precision=highest)
    queries = both_ways(mixed_qkv[:, 0] + qkv_bias[0] * live_cols)
    key_in = both_ways(mixed_qkv[:, 1])
    values = both_ways(mixed_qkv[:, 2] + qkv_bias[1] * live_cols)
    seq_shape = (SEQS, LEN, HP * HD)
    head_out = lax.map(jax.checkpoint(attend_one), (queries.reshape(seq_shape), key_in.reshape(seq_shape), values.reshape(seq_shape), seg_ids))
    head_out = both_ways(head_out.reshape(TOKENS, HP * HD))
    attn_out = low_back(jnp.dot(head_out, w_proj * live_cols[:, None], precision=highest) + proj_bias)
    residual = stream + attn_out
    entry_two = low(layer_norm(residual, gain_second, shift_second))
    pre_act = low_back(jnp.dot(entry_two, w_up, precision=highest) + up_bias)
    activation = low(jax.nn.gelu(pre_act, approximate=True))
    return residual + jnp.dot(activation, w_down, precision=highest) + down_bias

def reference(stream_in, seg_ids, gain_first, shift_first, w_qkv, qkv_bias, w_proj, proj_bias, gain_second, shift_second, w_up, up_bias, w_down, down_bias, cotangent):
    float_args = (stream_in.astype(jnp.float32), gain_first.astype(jnp.float32), shift_first.astype(jnp.float32), w_qkv.astype(jnp.float32), qkv_bias.astype(jnp.float32), w_proj.astype(jnp.float32), proj_bias.astype(jnp.float32), gain_second.astype(jnp.float32), shift_second.astype(jnp.float32), w_up.astype(jnp.float32), up_bias.astype(jnp.float32), w_down.astype(jnp.float32), down_bias.astype(jnp.float32))

    def forward_run(*arrays):
        return forward(*arrays, seg_ids)
    block_val, pullback = jax.vjp(forward_run, *float_args)
    gradients = pullback(cotangent.astype(jnp.float32))
    return (block_val.astype(jnp.bfloat16), gradients[0], gradients[1], gradients[2], gradients[3], gradients[4], gradients[5], gradients[6], gradients[7], gradients[8], gradients[9], gradients[10], gradients[11], gradients[12])
```

```python
import jax
import jax.numpy as jnp
from jax import lax
from jax.sharding import PartitionSpec as P

D = 1600
NH = 25
HD = 64
LANES = 128
epsilon = 1e-05
LOW = jnp.bfloat16


def flip(value, axis, bit):
    size = lax.axis_size(axis)
    return lax.ppermute(value, axis, [(i, i ^ bit) for i in range(size)])


def bits_of(axis):
    size, bit, found = lax.axis_size(axis), 1, []
    while bit < size:
        found.append(bit)
        bit *= 2
    return found


def my_sum(value):
    for bit in bits_of("my"):
        value = value + flip(value, "my", bit)
    return value


def mask_place(mask):
    return (mask & 1) * 2 + (mask >> 1)


def my_scatter(near, far):
    got = flip(far.astype(LOW), "my", 1).astype(jnp.float32)
    rows = near.shape[0] // 2
    across = flip((near[rows:] + got[rows:]).astype(LOW), "my", 2)
    return near[:rows] + got[:rows] + across.astype(jnp.float32)


def my_gather(block):
    near = jnp.concatenate([block, flip(block, "my", 2)], axis=0)
    return near, flip(near, "my", 1)


def stream_gather(value, axis):
    count, size = lax.axis_size("my"), lax.axis_size("mx")
    half = value.shape[axis]
    rows = half * size // count
    me = lax.axis_index("my")
    if size == 2 and half % rows == 0:
        whole = jnp.concatenate([value, flip(value, "mx", 1)], axis=axis)
        there = lax.axis_index("mx")

        def place(b):
            start = b * rows
            return ((start // half) ^ there) * half + start % half
    else:
        whole = lax.all_gather(value, "mx", axis=axis, tiled=True)

        def place(b):
            return b * rows

    def block(mask):
        return lax.dynamic_slice_in_dim(whole, place(me ^ mask), rows, axis=axis)

    return (
        jnp.concatenate([block(0), block(2)], axis=axis),
        jnp.concatenate([block(1), block(3)], axis=axis),
    )


def stream_scatter(near, far):
    count, size = lax.axis_size("my"), lax.axis_size("mx")
    rows = near.shape[0] // 2
    whole = jnp.concatenate([near, far], axis=0)
    me = lax.axis_index("my")

    def piece(b):
        return lax.dynamic_slice_in_dim(whole, mask_place(b ^ me) * rows, rows, axis=0)

    if size == 2:
        here = lax.axis_index("mx")
        per = count // 2
        send = jnp.concatenate([piece((1 - here) * per + i) for i in range(per)], axis=0)
        got = flip(send.astype(LOW), "mx", 1).astype(jnp.float32)
        return jnp.concatenate([piece(here * per + i) for i in range(per)], axis=0) + got
    ordered = jnp.concatenate([piece(b) for b in range(count)], axis=0)
    return lax.psum_scatter(
        ordered.astype(LOW), "mx", scatter_dimension=0, tiled=True
    ).astype(jnp.float32)


def dp_sum(value, kind=LOW):
    f32 = jnp.float32
    if lax.axis_size("dp") != 4:
        return lax.psum(value.astype(kind), "dp").astype(f32)
    half = value.shape[0] // 2
    here = lax.axis_index("dp")
    value = value.astype(kind)
    pair = value.astype(f32) + lax.ppermute(value, "dp", [(0, 1), (3, 2)]).astype(f32)
    first = here == 1
    send = jnp.where(first, pair[half:], pair[:half]).astype(kind)
    keep = jnp.where(first, pair[:half], pair[half:])
    mine = (keep + lax.ppermute(send, "dp", [(1, 2), (2, 1)]).astype(f32)).astype(kind)
    other = lax.ppermute(mine, "dp", [(1, 2), (2, 1)])
    whole = jnp.concatenate(
        [jnp.where(first, mine, other), jnp.where(first, other, mine)], axis=0
    )
    back = lax.ppermute(whole, "dp", [(1, 0), (2, 3)])
    return jnp.where((here == 1) | (here == 2), whole, back).astype(f32)


def pieces(width, wanted):
    if width % LANES or width // LANES < wanted:
        return [(0, width)]
    tiles = width // LANES
    ends = [LANES * (tiles * i // wanted) for i in range(wanted + 1)]
    return list(zip(ends[:-1], ends[1:]))


def rows_dot(left, right):
    return jnp.dot(left, right, preferred_element_type=jnp.float32)


def dot_wide(left, right):
    return lax.dot_general(left, right, (((1,), (1,)), ((), ())), preferred_element_type=jnp.float32)


def dot_tokens(left, right):
    return lax.dot_general(left, right, (((0,), (0,)), ((), ())), preferred_element_type=jnp.float32)


def both_dot(lefts, rights):
    return sum(dot_tokens(left, right) for left, right in zip(lefts, rights))


def visible(segment):
    position = jnp.arange(segment.shape[0])
    return (position[:, None] >= position[None, :]) & (segment[:, None] == segment[None, :])


def masked_scores(queries, key_in, segment):
    scores = jnp.einsum("qhd,khd->hqk", queries, key_in, preferred_element_type=jnp.float32)
    scores = scores * queries.shape[2] ** (-0.5)
    return jnp.where(visible(segment)[None], scores, -jnp.inf)


def attend_forward(queries, key_in, values, segment):
    scores = masked_scores(queries, key_in, segment)
    row_top = jnp.max(scores, axis=2, keepdims=True)
    exponent = jnp.exp(scores - row_top)
    row_total = jnp.sum(exponent, axis=2, keepdims=True)
    attn_weights = (exponent / row_total).astype(LOW)
    attended = jnp.einsum("hqk,khd->qhd", attn_weights, values, preferred_element_type=jnp.float32)
    return attended, row_top[:, :, 0] + jnp.log(row_total[:, :, 0])


def attend_back(queries, key_in, values, segment, log_totals, grad_heads):
    scores = masked_scores(queries, key_in, segment)
    soft_weights = jnp.exp(scores - log_totals[:, :, None])
    grad_weights = jnp.einsum(
        "qhd,khd->hqk", grad_heads, values, preferred_element_type=jnp.float32
    )
    grad_value = jnp.einsum(
        "hqk,qhd->khd", soft_weights.astype(LOW), grad_heads, preferred_element_type=jnp.float32
    )
    row_dot = jnp.sum(soft_weights * grad_weights, axis=2, keepdims=True)
    grad_scores = (soft_weights * (grad_weights - row_dot)).astype(LOW)
    score_scale = queries.shape[2] ** (-0.5)
    grad_query = (
        jnp.einsum("hqk,khd->qhd", grad_scores, key_in, preferred_element_type=jnp.float32)
        * score_scale
    )
    grad_key = (
        jnp.einsum("hqk,qhd->khd", grad_scores, queries, preferred_element_type=jnp.float32)
        * score_scale
    )
    return grad_query, grad_key, grad_value


def gelu_tanh(inputs):
    return jax.nn.gelu(inputs, approximate=True)


def row_stats(stream):
    totals = my_sum(jnp.stack([jnp.sum(stream, axis=1), jnp.sum(stream * stream, axis=1)]))
    row_mean = totals[0] / D
    spread = totals[1] / D - row_mean * row_mean
    return row_mean, lax.rsqrt(spread + epsilon)


def norm_back(grad_in, normed, rscale, gain_vec):
    scaled = grad_in * gain_vec
    totals = my_sum(jnp.stack([jnp.sum(scaled, axis=1), jnp.sum(scaled * normed, axis=1)]))
    return rscale[:, None] * (scaled - totals[0][:, None] / D - normed * (totals[1][:, None] / D))


def shards(
    stream_in,
    seg_ids,
    gain_first,
    shift_first,
    w_qkv,
    qkv_bias,
    w_proj,
    proj_bias,
    gain_second,
    shift_second,
    w_up,
    up_bias,
    w_down,
    down_bias,
    cotangent,
):
    f32 = jnp.float32
    head_cols = w_qkv.shape[2]
    local_heads = head_cols // HD
    width_rows = w_qkv.shape[0]
    hidden = w_up.shape[1]
    columns = lax.axis_index("mx") * head_cols + jnp.arange(head_cols)
    live_cols = (columns // HD < NH).astype(f32)
    live_low = live_cols.astype(LOW)
    groups = pieces(head_cols, 2)
    chunks = pieces(hidden, 3)

    w_groups = [
        jnp.concatenate([w_qkv[:, j, a:b] * live_low[a:b] for j in range(3)], axis=1)
        for a, b in groups
    ]
    w_proj_t = (w_proj * live_low[:, None]).T
    w_down_t = w_down.T

    raw_rows = stream_gather(stream_in, 0)
    cot_rows = stream_gather(cotangent, 0)
    stream = stream_in.astype(f32)
    mean_one, rscale_one = row_stats(stream)
    normed_one = (stream - mean_one[:, None]) * rscale_one[:, None]
    stats = stream_gather(jnp.stack([mean_one, rscale_one]), 1)
    rows_one = [
        (
            (raw.astype(f32) - stat[0][:, None]) * stat[1][:, None] * gain_first + shift_first
        ).astype(LOW)
        for raw, stat in zip(raw_rows, stats)
    ]

    per_seq = seg_ids.shape
    saved, rows_heads = [], []
    attn_out = [0.0, 0.0]
    for (a, b), w_group in zip(groups, w_groups):
        wide = b - a
        mixed = my_scatter(*[rows_dot(rows, w_group) for rows in rows_one])
        queries = (mixed[:, :wide] + (qkv_bias[0] * live_cols)[a:b]).astype(LOW)
        key_in = mixed[:, wide : 2 * wide].astype(LOW)
        values = (mixed[:, 2 * wide :] + (qkv_bias[1] * live_cols)[a:b]).astype(LOW)
        shape = (*per_seq, wide // HD, HD)
        block = (queries.reshape(shape), key_in.reshape(shape), values.reshape(shape), seg_ids)
        head_out, log_totals = jax.vmap(attend_forward)(*block)
        saved.append((*block, log_totals))
        rows_heads.append(my_gather(head_out.reshape(-1, wide).astype(LOW)))
        attn_out = [s + dot_wide(r, w_proj_t[:, a:b]) for s, r in zip(attn_out, rows_heads[-1])]
    attn_out = stream_scatter(*attn_out)

    grad_acts = [
        my_scatter(*[rows_dot(rows, w_down_t[:, a:b]) for rows in cot_rows]) for a, b in chunks
    ]

    residual = stream + attn_out + proj_bias
    mean_two, rscale_two = row_stats(residual)
    normed_two = (residual - mean_two[:, None]) * rscale_two[:, None]
    entry_two = (normed_two * gain_second + shift_second).astype(LOW)
    rows_two = stream_gather(entry_two, 0)

    acts, grad_pres, rows_pre = [], [], []
    for (a, b), grad_act in zip(chunks, grad_acts):
        pre_act = my_scatter(*[rows_dot(rows, w_up[:, a:b]) for rows in rows_two])
        activation, gelu_pull = jax.vjp(gelu_tanh, pre_act + up_bias[a:b])
        grad_pres.append(gelu_pull(grad_act)[0].astype(LOW))
        acts.append(activation.astype(LOW))
        rows_pre.append(my_gather(grad_pres[-1]))
    grad_up_bias = jnp.concatenate([jnp.sum(g, axis=0, dtype=f32) for g in grad_pres])

    grad_entry_two, grad_w_up = [0.0, 0.0], []
    for (a, b), rows in zip(chunks, rows_pre):
        grad_entry_two = [s + dot_wide(r, w_up[:, a:b]) for s, r in zip(grad_entry_two, rows)]
        grad_w_up.append(dp_sum(both_dot(rows_two, rows)))
    grad_w_up = jnp.concatenate(grad_w_up, axis=1)
    grad_entry_two = stream_scatter(*grad_entry_two)

    mlp_out, grad_w_down = [0.0, 0.0], []
    for (a, b), act in zip(chunks, acts):
        rows = my_gather(act)
        mlp_out = [s + dot_wide(r, w_down_t[:, a:b]) for s, r in zip(mlp_out, rows)]
        grad_w_down.append(dp_sum(both_dot(cot_rows, rows)))
    grad_w_down = jnp.concatenate(grad_w_down, axis=1).T
    block_out = (residual + stream_scatter(*mlp_out) + down_bias).astype(LOW)

    cot_own = cotangent.astype(f32)
    gain_two_part = jnp.sum(grad_entry_two * normed_two, axis=0)
    shift_two_part = jnp.sum(grad_entry_two, axis=0)
    grad_resid = norm_back(grad_entry_two, normed_two, rscale_two, gain_second) + cot_own
    grad_attn = grad_resid.astype(LOW)
    attn_rows = stream_gather(grad_attn, 0)
    grad_w_proj = jnp.concatenate([both_dot(attn_rows, rows) for rows in rows_heads], axis=1)
    grad_w_proj = (dp_sum(grad_w_proj) * live_cols).T

    rows_qkv, bias_sums = [], []
    for (a, b), block in zip(groups, saved):
        grad_heads = my_scatter(*[rows_dot(rows, w_proj_t[:, a:b]) for rows in attn_rows])
        grads = jax.vmap(attend_back)(
            *block, grad_heads.astype(LOW).reshape(block[0].shape)
        )
        low = jnp.concatenate([g.reshape(-1, b - a).astype(LOW) for g in grads], axis=1)
        rows_qkv.append(my_gather(low))
        bias_sums.append(jnp.sum(low, axis=0, dtype=f32))
    grad_entry_one, grad_w_qkv = [0.0, 0.0], []
    for rows, w_group, (a, b) in zip(rows_qkv, w_groups, groups):
        grad_entry_one = [s + dot_wide(r, w_group) for s, r in zip(grad_entry_one, rows)]
        wide = b - a
        grad_w_qkv.append(
            [
                dp_sum(both_dot(rows_one, [r[:, j * wide : (j + 1) * wide] for r in rows]))
                * live_cols[a:b]
                for j in range(3)
            ]
        )
    grad_entry_one = stream_scatter(*grad_entry_one)
    grad_w_qkv = jnp.stack(
        [jnp.concatenate([g[j] for g in grad_w_qkv], axis=1) for j in range(3)], axis=1
    )
    gain_one_part = jnp.sum(grad_entry_one * normed_one, axis=0)
    shift_one_part = jnp.sum(grad_entry_one, axis=0)
    grad_stream = norm_back(grad_entry_one, normed_one, rscale_one, gain_first) + grad_resid

    query_bias = jnp.concatenate([s[: b - a] for s, (a, b) in zip(bias_sums, groups)]) * live_cols
    value_bias = (
        jnp.concatenate([s[2 * (b - a) :] for s, (a, b) in zip(bias_sums, groups)]) * live_cols
    )
    token_sums = dp_sum(my_sum(jnp.concatenate([grad_up_bias, query_bias, value_bias])), f32)
    grad_up_bias = token_sums[:hidden]
    grad_qkv_bias = token_sums[hidden:].reshape(2, head_cols)
    stream_sums = jnp.stack(
        [
            gain_one_part,
            shift_one_part,
            gain_two_part,
            shift_two_part,
            jnp.sum(grad_attn, axis=0, dtype=f32),
            jnp.sum(cot_own, axis=0),
        ]
    )
    for bit in bits_of("mx"):
        stream_sums = stream_sums + flip(stream_sums, "mx", bit)
    (
        grad_gain_first,
        grad_shift_first,
        grad_gain_second,
        grad_shift_second,
        grad_proj_bias,
        grad_down_bias,
    ) = dp_sum(stream_sums, f32)
    return (
        block_out,
        grad_stream,
        grad_gain_first,
        grad_shift_first,
        grad_w_qkv,
        grad_qkv_bias,
        grad_w_proj,
        grad_proj_bias,
        grad_gain_second,
        grad_shift_second,
        grad_w_up,
        grad_up_bias,
        grad_w_down,
        grad_down_bias,
    )


def solution(mesh):
    return jax.shard_map(
        shards,
        mesh=mesh,
        in_specs=(
            P(("dp", "mx"), "my"),
            P(("dp", "my"), None),
            P("my"),
            P("my"),
            P("my", None, "mx"),
            P(None, "mx"),
            P("mx", "my"),
            P("my"),
            P("my"),
            P("my"),
            P("my", "mx"),
            P("mx"),
            P("mx", "my"),
            P("my"),
            P(("dp", "mx"), "my"),
        ),
        out_specs=(
            P(("dp", "mx"), "my"),
            P(("dp", "mx"), "my"),
            P("my"),
            P("my"),
            P("my", None, "mx"),
            P(None, "mx"),
            P("mx", "my"),
            P("my"),
            P("my"),
            P("my"),
            P("my", "mx"),
            P("mx"),
            P("mx", "my"),
            P("my"),
        ),
        check_vma=False,
    )
```
